32 devices in a mesh: scen: 16 (over z, y, core), net: 2 (over x).
Axes of the slice: x: 2, y: 2, z: 4, core: 2. Of those that a mesh axis runs over, the one named last changes fastest.
Arguments:
- generation: float32 [16, 168, 4096], P('scen', None, 'net'), may hold values from 0 to 2
- charging: float32 [16, 168, 1024], P('scen', None, 'net'), may hold values from 0 to 0.5
- discharging: float32 [16, 168, 1024], P('scen', None, 'net'), may hold values from 0 to 0.5
- plant_capacity: float32 [4096], P('net'), may hold values from 1 to 3
- store_capacity: float32 [1024], P('net'), may hold values from 4 to 12
- dual_balance: float32 [16, 168], P('scen'), may hold values from -6 to 6
- dual_line: float32 [16, 168, 8192], P('scen', None, 'net'), may hold values from -6 to 6
- dual_headroom: float32 [16, 168, 4096], P('scen', None, 'net'), may hold values from 0 to 1
- dual_empty: float32 [16, 168, 1024], P('scen', None, 'net'), may hold values from -1 to 0
- dual_full: float32 [16, 168, 1024], P('scen', None, 'net'), may hold values from 0 to 1
- availability: float32 [16, 168, 4096], P('scen', None, 'net'), may hold values from 0.1 to 1
- demand: float32 [16, 168], P('scen'), may hold values from 0.5 to 1.5
- line_base: float32 [16, 168, 8192], P('scen', None, 'net'), may hold values from -6 to 6
- line_limit: float32 [8192], P('net'), may hold values from 0.5 to 2
- fuel_cost: float32 [4096], P('net'), may hold values from 0.1 to 2
- plant_cost: float32 [4096], P('net'), may hold values from 0.1 to 1
- store_cost: float32 [1024], P('net'), may hold values from 0.05 to 0.5
- self_loss: float32 [1024], P('net'), may hold values from 0.002 to 0.05
- power_limit: float32 [1024], P('net'), may hold values from 0.5 to 2
- store_node: int32 [1024], P('net'), may hold values from 0 to 4095, as said below
- line_factors: float32 [16, 512, 10, 256], P('net', 'scen'), may hold values from -0.125 to 0.125
- block_pattern: int32 [16, 10], P('net'), may hold values from 0 to 15, as said below
Outputs:
- next_generation: float32 [16, 168, 4096], P('scen', None, 'net')
- next_charging: float32 [16, 168, 1024], P('scen', None, 'net')
- next_discharging: float32 [16, 168, 1024], P('scen', None, 'net')
- next_plant: float32 [4096], P('net')
- next_store: float32 [1024], P('net')
- next_balance: float32 [16, 168], P('scen')
- next_line: float32 [16, 168, 8192], P('scen', None, 'net')
- next_headroom: float32 [16, 168, 4096], P('scen', None, 'net')
- next_empty: float32 [16, 168, 1024], P('scen', None, 'net')
- next_full: float32 [16, 168, 1024], P('scen', None, 'net')
The draws below stay inside these ranges and needn't reach their ends.
Inputs may be any that keep to these rules, and one draw needn't show every extreme that they name: `store_node`: storage unit k sits at a node of block k // 64. `block_pattern`: row b lists 10 different node blocks, the first of them b itself.
All inputs are finite; a program needn't handle non-finite values.
Results may differ from the reference program's by a relative error of at most 0.00016.
Values sent between devices are 32-bit elements; how exact they have to be, the bound alone decides.
A program may use at most 128 MiB of HBM per device.

```python
import math
import jax
import jax.numpy as jnp
from jax import lax

HOURS = 168
BLOCKS = 16
BLOCK = 256
BPAT = 10
GLINES = 512
STORE_BLK = 64
SCEN = 16
NODES = 4096
LINES = 8192
STORES = 1024


def draw_store_node(key, part):
    offsets = jax.random.randint(jax.random.fold_in(key, 7), (STORES,), 0, BLOCK)
    owners = jnp.arange(STORES, dtype=jnp.int32) // STORE_BLK
    placed = owners * BLOCK + offsets.astype(jnp.int32)
    placed = placed.at[0].set(0).at[STORES - 1].set(NODES - 1)
    return placed.astype(jnp.int32)


def draw_block_pattern(key, part):
    row_keys = jax.random.split(jax.random.fold_in(key, 11), BLOCKS)

    def one_row(row_key, own_block):
        ordering = jax.random.permutation(row_key, BLOCKS - 1)[:BPAT - 1].astype(jnp.int32)
        others = jnp.where(ordering >= own_block, ordering + 1, ordering)
        return jnp.concatenate([own_block[None], others]).astype(jnp.int32)
    return jax.vmap(one_row)(row_keys, jnp.arange(BLOCKS, dtype=jnp.int32))


def level_of(rng, extent, cuts, smallest, high):
    gain, own = 1.0, jax.random.fold_in(rng, 6)
    for position, parts in cuts:
        draws = jnp.exp(jax.random.uniform(jax.random.fold_in(own, position), (parts,), jnp.float32, smallest / len(cuts), high / len(cuts)))
        gain = gain * jnp.repeat(draws, extent[position] // parts).reshape([-1 if axis == position else 1 for axis in range(len(extent))])
    return gain


def gaussian(stream_key, extent, spread, limit, cuts=(), held_as=jnp.bfloat16):
    factor_of = level_of(stream_key, extent, cuts, -0.22, 0.18) if cuts else 1.0
    entries = jax.random.normal(stream_key, extent, jnp.float32) * spread * factor_of
    return jnp.minimum(jnp.maximum(entries, -limit), limit).astype(held_as)


def setup_inputs(seed: int = 0) -> dict:
    key_list = jax.random.split(jax.random.key(seed), 23)
    return {
        "generation": jnp.clip(2.0 * jax.random.uniform(key_list[0], (SCEN, HOURS, NODES), jnp.float32) ** level_of(key_list[0], (SCEN, HOURS, NODES), ((0, 16), (2, 2)), -0.2, 0.2), 0.0, 2.0),
        "charging": jnp.clip(0.5 * jax.random.uniform(key_list[1], (SCEN, HOURS, STORES), jnp.float32) ** level_of(key_list[1], (SCEN, HOURS, STORES), ((0, 16), (2, 2)), -0.2, 0.2), 0.0, 0.5),
        "discharging": jnp.clip(0.5 * jax.random.uniform(key_list[2], (SCEN, HOURS, STORES), jnp.float32) ** level_of(key_list[2], (SCEN, HOURS, STORES), ((0, 16), (2, 2)), -0.2, 0.2), 0.0, 0.5),
        "plant_capacity": jnp.clip(1.0 + 2.0 * jax.random.uniform(key_list[3], (NODES,), jnp.float32) ** level_of(key_list[3], (NODES,), ((0, 2),), -0.2, 0.2), 1.0, 3.0),
        "store_capacity": jnp.clip(4.0 + 8.0 * jax.random.uniform(key_list[4], (STORES,), jnp.float32) ** level_of(key_list[4], (STORES,), ((0, 2),), -0.2, 0.2), 4.0, 12.0),
        "dual_balance": gaussian(key_list[5], (SCEN, HOURS), 1.0, 6.0, ((0, 16),), jnp.float32),
        "dual_line": gaussian(key_list[6], (SCEN, HOURS, LINES), 1.0, 6.0, ((0, 16), (2, 2)), jnp.float32),
        "dual_headroom": jnp.clip(1.0 * jax.random.uniform(key_list[7], (SCEN, HOURS, NODES), jnp.float32) ** level_of(key_list[7], (SCEN, HOURS, NODES), ((0, 16), (2, 2)), -0.2, 0.2), 0.0, 1.0),
        "dual_empty": jnp.clip(-1.0 + 1.0 * jax.random.uniform(key_list[8], (SCEN, HOURS, STORES), jnp.float32) ** level_of(key_list[8], (SCEN, HOURS, STORES), ((0, 16), (2, 2)), -0.2, 0.2), -1.0, 0.0),
        "dual_full": jnp.clip(1.0 * jax.random.uniform(key_list[9], (SCEN, HOURS, STORES), jnp.float32) ** level_of(key_list[9], (SCEN, HOURS, STORES), ((0, 16), (2, 2)), -0.2, 0.2), 0.0, 1.0),
        "availability": jnp.clip(0.1 + 0.9 * jax.random.uniform(key_list[10], (SCEN, HOURS, NODES), jnp.float32) ** level_of(key_list[10], (SCEN, HOURS, NODES), ((0, 16), (2, 2)), -0.2, 0.2), 0.1, 1.0),
        "demand": jnp.clip(0.5 + 1.0 * jax.random.uniform(key_list[11], (SCEN, HOURS), jnp.float32) ** level_of(key_list[11], (SCEN, HOURS), ((0, 16),), -0.2, 0.2), 0.5, 1.5),
        "line_base": gaussian(key_list[12], (SCEN, HOURS, LINES), 1.0, 6.0, ((0, 16), (2, 2)), jnp.float32),
        "line_limit": jnp.clip(0.5 + 1.5 * jax.random.uniform(key_list[13], (LINES,), jnp.float32) ** level_of(key_list[13], (LINES,), ((0, 2),), -0.2, 0.2), 0.5, 2.0),
        "fuel_cost": jnp.clip(jnp.exp(math.log(2.0) - 2.9957323 * jax.random.uniform(key_list[14], (NODES,), jnp.float32) ** level_of(key_list[14], (NODES,), ((0, 2),), -0.2, 0.2)), 0.1, 2.0),
        "plant_cost": jnp.clip(jnp.exp(math.log(1.0) - 2.3025851 * jax.random.uniform(key_list[15], (NODES,), jnp.float32) ** level_of(key_list[15], (NODES,), ((0, 2),), -0.2, 0.2)), 0.1, 1.0),
        "store_cost": jnp.clip(jnp.exp(math.log(0.5) - 2.3025851 * jax.random.uniform(key_list[16], (STORES,), jnp.float32) ** level_of(key_list[16], (STORES,), ((0, 2),), -0.2, 0.2)), 0.05, 0.5),
        "self_loss": jnp.clip(jnp.exp(math.log(0.05) - 3.218876 * jax.random.uniform(key_list[17], (STORES,), jnp.float32) ** level_of(key_list[17], (STORES,), ((0, 2),), -0.2, 0.2)), 0.002, 0.05),
        "power_limit": jnp.clip(0.5 + 1.5 * jax.random.uniform(key_list[18], (STORES,), jnp.float32) ** level_of(key_list[18], (STORES,), ((0, 2),), -0.2, 0.2), 0.5, 2.0),
        "store_node": draw_store_node(jax.random.fold_in(key_list[22], 71), 0),
        "line_factors": gaussian(key_list[20], (BLOCKS, GLINES, BPAT, BLOCK), (BPAT * BLOCK) ** -0.5, 0.125, ((0, 2), (1, 16)), jnp.float32),
        "block_pattern": draw_block_pattern(jax.random.fold_in(key_list[22], 71), 0),
    }


highest = lax.Precision.HIGHEST
primal_step = 0.5
dual_step = 0.5
store_step = 0.05
level_step = 0.05
efficiency = 0.92


def line_dual_image(dual_line, line_factors, block_pattern):
    rows_all = SCEN * HOURS
    grouped_duals = dual_line.reshape(rows_all, BLOCKS, GLINES)

    def add_group(carry_image, group_index):
        factors = line_factors[group_index].reshape(GLINES, BPAT * BLOCK)
        line_duals = lax.dynamic_index_in_dim(grouped_duals, group_index, 1, keepdims=False)
        contribution = jnp.dot(line_duals, factors, precision=highest, preferred_element_type=jnp.float32)
        carry_image = carry_image.at[:, block_pattern[group_index], :].add(contribution.reshape(rows_all, BPAT, BLOCK))
        return carry_image, None

    initial = jnp.zeros((rows_all, BLOCKS, BLOCK), jnp.float32)
    nodal_image = lax.scan(add_group, initial, jnp.arange(BLOCKS, dtype=jnp.int32))[0]
    return nodal_image.reshape(SCEN, HOURS, NODES)


def flow_rows(injection, line_factors, block_pattern):
    rows_all = SCEN * HOURS
    blocks_all = injection.reshape(rows_all, BLOCKS, BLOCK)

    def one_group(group_index):
        chosen = blocks_all[:, block_pattern[group_index], :].reshape(rows_all, BPAT * BLOCK)
        factors = line_factors[group_index].reshape(GLINES, BPAT * BLOCK)
        return jnp.dot(chosen, factors.T, precision=highest, preferred_element_type=jnp.float32)

    outputs = lax.map(one_group, jnp.arange(BLOCKS, dtype=jnp.int32))
    return jnp.transpose(outputs, (1, 0, 2)).reshape(SCEN, HOURS, BLOCKS * GLINES)


def charge_levels(charge_drive, keep_rate):
    def advance(level_now, column):
        level_now = keep_rate * level_now + column
        return level_now, level_now

    initial = jnp.zeros((charge_drive.shape[0], charge_drive.shape[2]), jnp.float32)
    levels = lax.scan(advance, initial, jnp.transpose(charge_drive, (1, 0, 2)))[1]
    return jnp.transpose(levels, (1, 0, 2))


def charge_adjoint(weights, keep_rate):
    def retreat(level_now, column):
        level_now = keep_rate * level_now + column
        return level_now, level_now

    initial = jnp.zeros((weights.shape[0], weights.shape[2]), jnp.float32)
    levels = lax.scan(retreat, initial, jnp.transpose(weights, (1, 0, 2)), reverse=True)[1]
    return jnp.transpose(levels, (1, 0, 2))


def reference(generation, charging, discharging, plant_capacity, store_capacity, dual_balance, dual_line, dual_headroom, dual_empty, dual_full, availability, demand, line_base, line_limit, fuel_cost, plant_cost, store_cost, self_loss, power_limit, store_node, line_factors, block_pattern):
    keep_rate = 1.0 - self_loss
    line_image = line_dual_image(dual_line, line_factors, block_pattern)
    nodal_price = dual_balance[:, :, None] + line_image
    backward = charge_adjoint(dual_empty + dual_full, keep_rate)
    next_generation = jnp.maximum(generation - primal_step * (fuel_cost + nodal_price + dual_headroom), 0.0)
    store_price = nodal_price[:, :, store_node]
    next_charging = jnp.clip(charging - store_step * (efficiency * backward - store_price), 0.0, power_limit)
    next_discharging = jnp.clip(discharging - store_step * (store_price - backward / efficiency), 0.0, power_limit)
    plant_total = jnp.sum(availability * dual_headroom, axis=(0, 1))
    store_total = jnp.sum(dual_full, axis=(0, 1))
    next_plant = jnp.maximum(plant_capacity - primal_step * (plant_cost - plant_total / (SCEN * HOURS)), 0.0)
    next_store = jnp.maximum(store_capacity - primal_step * (store_cost - store_total / (SCEN * HOURS)), 0.0)
    extra_generation = 2.0 * next_generation - generation
    extra_charging = 2.0 * next_charging - charging
    extra_discharging = 2.0 * next_discharging - discharging
    extra_plant = 2.0 * next_plant - plant_capacity
    extra_store = 2.0 * next_store - store_capacity
    injection = extra_generation.at[:, :, store_node].add(extra_discharging - extra_charging)
    next_balance = dual_balance + dual_step * (jnp.sum(injection, axis=2) / NODES - demand)
    line_flows = flow_rows(injection, line_factors, block_pattern)
    line_moved = dual_line + dual_step * line_flows
    next_line = line_moved - dual_step * jnp.clip(line_moved / dual_step, -line_limit - line_base, line_limit - line_base)
    next_headroom = jnp.maximum(dual_headroom + dual_step * (extra_generation - availability * extra_plant), 0.0)
    levels = charge_levels(efficiency * extra_charging - extra_discharging / efficiency, keep_rate)
    next_empty = jnp.minimum(dual_empty + level_step * levels, 0.0)
    next_full = jnp.maximum(dual_full + level_step * (levels - extra_store), 0.0)
    return (next_generation, next_charging, next_discharging, next_plant, next_store, next_balance, next_line, next_headroom, next_empty, next_full)
```

```python
import functools

import jax
import jax.numpy as jnp
from jax import lax
from jax.experimental import pallas as pl
from jax.experimental.pallas import tpu as pltpu
from jax.sharding import PartitionSpec as P

LANES = 128
primal_step = 0.5
dual_step = 0.5
store_step = 0.05
level_step = 0.05
efficiency = 0.92
f32 = jnp.float32
bf16 = jnp.bfloat16
VMEM_BYTES = 56 * 1024 * 1024


def split(x):
    hi = x.astype(bf16)
    return hi, (x - hi.astype(f32)).astype(bf16)


def stacked(x):
    return jnp.concatenate([x, x - x.astype(bf16).astype(f32)], axis=0).astype(bf16)


def dot(a, b):
    return jnp.dot(a, b, preferred_element_type=f32)


def dot_t(a, b):
    return lax.dot_general(a, b, (((1,), (1,)), ((), ())), preferred_element_type=f32)


def slot_steps(slots):
    return [range(j, min(j + 2, slots)) for j in range(0, slots, 2)]


def image_kernel(slots, parts, pat, dual, fac, *refs):
    outs, acc = refs[-1 - parts : -1], refs[-1]
    g = pl.program_id(0)
    hours = dual.shape[0]
    lines = fac.shape[0] * fac.shape[2]

    @pl.when(g == 0)
    def _():
        acc[...] = jnp.zeros_like(acc)

    both = stacked(dual[...])
    hi = dual[...].astype(bf16)
    for js in slot_steps(slots):
        w = fac[:, 0, :, js[0] * LANES : (js[-1] + 1) * LANES].reshape(lines, len(js) * LANES)
        wh, wl = split(w)
        r = dot(both, wh)
        r = r[:hours] + r[hours:] + dot(hi, wl)
        for i, j in enumerate(js):
            b = pat[g, j]
            acc[b] = acc[b] + r[:, i * LANES : (i + 1) * LANES]

    @pl.when(g == pl.num_programs(0) - 1)
    def _():
        own = outs[0].shape[0]
        for s in range(parts):
            outs[s][...] = acc[s * own : (s + 1) * own]


def image_parts(pattern, dual, fac, parts, after):
    groups, slots = pattern.shape
    hours = dual.shape[0]
    scen, _, lines_local, width = fac.shape
    lines = scen * lines_local
    full = jax.ShapeDtypeStruct((groups, hours, LANES), f32)
    whole = pl.BlockSpec((groups, hours, LANES), lambda g, pat: (0, 0, 0))
    return pl.pallas_call(
        functools.partial(image_kernel, slots, parts),
        out_shape=[full] * parts,
        grid_spec=pltpu.PrefetchScalarGridSpec(
            num_scalar_prefetch=1,
            grid=(groups,),
            in_specs=[
                pl.BlockSpec((hours, lines), lambda g, pat: (0, g)),
                pl.BlockSpec((scen, 1, lines_local, width), lambda g, pat: (0, g, 0, 0)),
            ]
            + [pl.BlockSpec(memory_space=pl.ANY)] * len(after),
            out_specs=[whole] * parts,
            scratch_shapes=[pltpu.VMEM((groups * parts, hours, LANES), f32)],
        ),
        compiler_params=pltpu.CompilerParams(vmem_limit_bytes=VMEM_BYTES),
        cost_estimate=pl.CostEstimate(
            flops=6 * groups * hours * lines * width,
            bytes_accessed=4 * groups * lines * width,
            transcendentals=0,
        ),
        name="image",
    )(pattern, dual, fac, *after)


def flow_kernel(slots, parts, first, last, pat, fac, *refs):
    injs, refs = refs[:parts], refs[parts:]
    if not first:
        prev, refs = refs[0], refs[1:]
    if last:
        dual, base, limit = refs[:3]
        refs = refs[3:]
    out, total, held = refs
    g = pl.program_id(0)
    own, hours, _ = injs[0].shape
    lines = fac.shape[0] * fac.shape[2]

    @pl.when(g == 0)
    def _():
        rows = jnp.zeros((hours, LANES), f32)
        for s in range(parts):
            for b in range(own):
                x = injs[s][b]
                held[s * own + b] = stacked(x)
                rows = rows + x
        total[...] = rows

    flows = jnp.zeros((hours, lines), f32) if first else prev[...]
    for js in slot_steps(slots):
        w = fac[:, 0, :, js[0] * LANES : (js[-1] + 1) * LANES].reshape(lines, len(js) * LANES)
        wh, wl = split(w)
        both = jnp.concatenate([held[pat[g, j]] for j in js], axis=1)
        hi = jnp.concatenate([held[pat[g, j], :hours] for j in js], axis=1)
        r = dot_t(both, wh)
        flows = flows + (r[:hours] + r[hours:] + dot_t(hi, wl))
    if last:
        moved = dual[...] + dual_step * flows
        low = -limit[...] - base[...]
        high = limit[...] - base[...]
        out[...] = moved - dual_step * jnp.minimum(jnp.maximum(moved / dual_step, low), high)
    else:
        out[...] = flows


def flow_step(pattern, fac, injs, prev, tail):
    groups, slots = pattern.shape
    parts = len(injs)
    hours = injs[0].shape[1]
    scen, _, lines_local, width = fac.shape
    lines = scen * lines_local
    by_group = pl.BlockSpec((hours, lines), lambda g, pat: (0, g))
    whole = pl.BlockSpec((groups, hours, LANES), lambda g, pat: (0, 0, 0))
    operands = list(injs)
    specs = [whole] * parts
    if prev is not None:
        operands.append(prev)
        specs.append(by_group)
    if tail is not None:
        operands += list(tail)
        specs += [by_group, by_group, pl.BlockSpec((1, lines), lambda g, pat: (0, g))]
    return pl.pallas_call(
        functools.partial(flow_kernel, slots, parts, prev is None, tail is not None),
        out_shape=[
            jax.ShapeDtypeStruct((hours, groups * lines), f32),
            jax.ShapeDtypeStruct((hours, LANES), f32),
        ],
        grid_spec=pltpu.PrefetchScalarGridSpec(
            num_scalar_prefetch=1,
            grid=(groups,),
            in_specs=[
                pl.BlockSpec((scen, 1, lines_local, width), lambda g, pat: (0, g, 0, 0)),
            ]
            + specs,
            out_specs=[by_group, pl.BlockSpec((hours, LANES), lambda g, pat: (0, 0))],
            scratch_shapes=[pltpu.VMEM((groups * parts, 2 * hours, LANES), bf16)],
        ),
        compiler_params=pltpu.CompilerParams(vmem_limit_bytes=VMEM_BYTES),
        cost_estimate=pl.CostEstimate(
            flops=6 * groups * hours * lines * width,
            bytes_accessed=4 * groups * lines * width,
            transcendentals=0,
        ),
        name="flows",
    )(pattern, fac, *operands)


def decayed_sums(x, keep, reverse):
    hours = x.shape[0]
    hour = lax.broadcasted_iota(jnp.int32, x.shape, 0)
    power = keep
    lag = 1
    while lag < hours:
        if reverse:
            moved = jnp.where(hour < hours - lag, pltpu.roll(x, hours - lag, 0), 0.0)
        else:
            moved = jnp.where(hour >= lag, pltpu.roll(x, lag, 0), 0.0)
        x = x + power * moved
        power = power * power
        lag *= 2
    return x


def adjoint_kernel(empty, full, loss, out):
    out[...] = decayed_sums(empty[...] + full[...], 1.0 - loss[...], True)


def level_kernel(charging, discharging, next_c, next_d, empty, full, loss, extra, out_e, out_f):
    extra_c = 2.0 * next_c[...] - charging[...]
    extra_d = 2.0 * next_d[...] - discharging[...]
    drive = efficiency * extra_c - extra_d / efficiency
    levels = decayed_sums(drive, 1.0 - loss[...], False)
    out_e[...] = jnp.minimum(empty[...] + level_step * levels, 0.0)
    out_f[...] = jnp.maximum(full[...] + level_step * (levels - extra[...]), 0.0)


def simple_call(kernel, out_shape, name, *operands):
    moved = sum(4 * x.size for x in operands) + sum(
        4 * x.size for x in jax.tree.leaves(out_shape)
    )
    return pl.pallas_call(
        kernel,
        out_shape=out_shape,
        compiler_params=pltpu.CompilerParams(vmem_limit_bytes=VMEM_BYTES),
        cost_estimate=pl.CostEstimate(flops=8 * moved, bytes_accessed=moved, transcendentals=0),
        name=name,
    )(*operands)


def dispatch_kernel(chunk, width, parts, store_blk, *refs):
    images, refs = refs[:parts], refs[parts:]
    (balance, generation, headroom, fuel, charging, discharging, backward, power, rows,
     price_in, gen_in, gen_out, inj, price_out, out_c, out_d) = refs
    groups = images[0].shape[0]
    per = LANES // store_blk
    gen_out[...] = gen_in[...]
    for t in range(groups // per):
        prices, extras = [], []
        for b in range(t * per, (t + 1) * per):
            cols = slice(b * width + chunk * LANES, b * width + (chunk + 1) * LANES)
            image = images[0][b]
            for other in images[1:]:
                image = image + other[b]
            price = balance[...] + image
            gen = generation[:, cols]
            moved = jnp.maximum(gen - primal_step * (fuel[:, cols] + price + headroom[:, cols]), 0.0)
            gen_out[:, cols] = moved
            prices.append(price)
            extras.append(2.0 * moved - gen)
        units = slice(t * LANES, (t + 1) * LANES)
        place = lax.broadcasted_iota(jnp.int32, (per * LANES, LANES), 0)
        marks = jnp.where(place == rows[:, units], 1.0, 0.0).astype(bf16)
        hi, lo = split(jnp.concatenate(prices, axis=1))
        price = price_in[:, units] + (dot(hi, marks) + dot(lo, marks))
        price_out[:, units] = price
        back = backward[:, units]
        cap = power[:, units]
        c, d = charging[:, units], discharging[:, units]
        next_c = jnp.minimum(jnp.maximum(c - store_step * (efficiency * back - price), 0.0), cap)
        next_d = jnp.minimum(jnp.maximum(d - store_step * (price - back / efficiency), 0.0), cap)
        out_c[:, units] = next_c
        out_d[:, units] = next_d
        hi, lo = split((2.0 * next_d - d) - (2.0 * next_c - c))
        spread = dot_t(hi, marks) + dot_t(lo, marks)
        for i in range(per):
            inj[t * per + i] = extras[i] + spread[:, i * LANES : (i + 1) * LANES]


def body(
    generation, charging, discharging, plant_capacity, store_capacity, dual_balance, dual_line,
    dual_headroom, dual_empty, dual_full, availability, demand, line_base, line_limit, fuel_cost,
    plant_cost, store_cost, self_loss, power_limit, store_node, line_factors, block_pattern,
):
    scen_rows, hours, node_local = generation.shape
    groups, lines_local, slots, width = line_factors.shape
    parts = lax.axis_size("net")
    scen_size = lax.axis_size("scen")
    block_count = groups * parts
    stores = store_node.shape[0]
    store_blk = stores // groups
    chunks = width // LANES
    me = lax.axis_index("net")

    gen, chg, dis = generation[0], charging[0], discharging[0]
    line, head = dual_line[0], dual_headroom[0]
    empty, full, avail = dual_empty[0], dual_full[0], availability[0]
    loss = self_loss[None, :]

    pattern = (block_pattern - me * groups + block_count) % block_count
    node = store_node - me * node_local
    unit = jnp.arange(stores, dtype=jnp.int32)
    per = LANES // store_blk
    pair_row = (node // width - (unit // LANES) * per) * LANES + node % LANES
    gathered = []
    for q in range(chunks):
        piece = line_factors[:, :, :, q * LANES : (q + 1) * LANES]
        piece = piece.reshape(groups, lines_local, slots * LANES)
        gathered.append(lax.all_gather(piece, "scen", axis=0))

    backward = simple_call(
        adjoint_kernel, jax.ShapeDtypeStruct((hours, stores), f32), "adjoint", empty, full, loss
    )
    plant_part = jnp.sum(avail * head, axis=0)
    store_part = jnp.sum(full, axis=0)
    totals = lax.psum(jnp.concatenate([plant_part, store_part]), "scen")
    plant_total, store_total = totals[:node_local], totals[node_local:]
    scen_hours = scen_rows * scen_size * hours
    next_plant = jnp.maximum(
        plant_capacity - primal_step * (plant_cost - plant_total / scen_hours), 0.0
    )
    next_store = jnp.maximum(
        store_capacity - primal_step * (store_cost - store_total / scen_hours), 0.0
    )
    extra_plant = 2.0 * next_plant - plant_capacity
    extra_store = 2.0 * next_store - store_capacity

    price = jnp.zeros((hours, stores), f32)
    next_gen = gen
    flows = None
    totals_by_lane = jnp.zeros((hours, LANES), f32)
    by_store = jax.ShapeDtypeStruct((hours, stores), f32)
    by_node = jax.ShapeDtypeStruct((hours, node_local), f32)
    for q in range(chunks):
        after = [totals, backward] if q == 0 else [flows]
        partial_images = image_parts(pattern, line, gathered[q], parts, after)
        images = [partial_images[0]]
        for s in range(1, parts):
            images.append(
                lax.ppermute(partial_images[s], "net", [(i, (i + s) % parts) for i in range(parts)])
            )
        rows = jnp.where((node % width) // LANES == q, pair_row, -1)[None, :]
        next_gen, inj, price, next_c, next_d = simple_call(
            functools.partial(dispatch_kernel, q, width, parts, store_blk),
            [by_node, jax.ShapeDtypeStruct((groups, hours, LANES), f32), by_store, by_store, by_store],
            "dispatch",
            *images, dual_balance[0][:, None], gen, head, fuel_cost[None, :], chg, dis, backward,
            power_limit[None, :], rows, price, next_gen,
        )
        injs = [inj]
        for s in range(1, parts):
            injs.append(lax.ppermute(inj, "net", [(i, (i - s) % parts) for i in range(parts)]))
        tail = (line, line_base[0], line_limit[None, :]) if q == chunks - 1 else None
        flows, sums = flow_step(pattern, gathered[q], injs, flows, tail)
        totals_by_lane = totals_by_lane + sums

    next_empty, next_full = simple_call(
        level_kernel, [by_store, by_store], "levels",
        chg, dis, next_c, next_d, empty, full, loss, extra_store[None, :],
    )
    extra_generation = 2.0 * next_gen - gen
    next_headroom = jnp.maximum(head + dual_step * (extra_generation - avail * extra_plant), 0.0)
    next_balance = dual_balance + dual_step * (
        jnp.sum(totals_by_lane, axis=1)[None] / (block_count * width) - demand
    )
    return (
        next_gen[None], next_c[None], next_d[None], next_plant, next_store, next_balance,
        flows[None], next_headroom[None], next_empty[None], next_full[None],
    )


def solution(mesh):
    row = P("scen", None, "net")
    placed = (
        row, row, row, P("net"), P("net"), P("scen", None), row, row, row, row, row,
        P("scen", None), row, P("net"), P("net"), P("net"), P("net"), P("net"), P("net"), P("net"),
        P("net", "scen", None, None), P("net", None),
    )
    return jax.shard_map(
        body,
        mesh=mesh,
        in_specs=placed,
        out_specs=(row, row, row, P("net"), P("net"), P("scen", None), row, row, row, row),
        check_vma=False,
    )
```
